32 devices in a mesh: shard: 4 (over x, core), context: 4 (over z), tensor: 2 (over y).
Axes of the slice: x: 2, y: 2, z: 4, core: 2. Of those that a mesh axis runs over, the one named last changes fastest.
Arguments:
- layer_input: bfloat16 [4, 2048, 1024], P('shard', 'context'), may hold values from -5 to 5
- segment_ids: int32 [4, 2048], P('shard'), may hold values from 0 to 3, never falling along the last dimension, each value on 1 to 1024 neighbouring positions
- out_grad: bfloat16 [4, 2048, 1024], P('shard', ('context', 'tensor')), may hold values from -6 to 6
- attn_in: float32 [3, 1024, 1024], P(None, 'shard', 'tensor'), may hold values from -0.1875 to 0.1875
- attn_out: float32 [1024, 1024], P('tensor', 'shard'), may hold values from -0.75 to 0.75
- mlp_up: float32 [1024, 4096], P('shard', 'tensor'), may hold values from -0.1875 to 0.1875
- mlp_down: float32 [4096, 1024], P('tensor', 'shard'), may hold values from -0.09375 to 0.09375
- vectors: float32 [8, 1024], replicated, may hold values from -0.8 to 1.4, as said below
- up_bias: float32 [4096], replicated, may hold values from -0.8 to 0.8
- attn_in_moments: float32 [2, 3, 1024, 1024], P(None, None, 'shard', 'tensor'), may hold values from -1.44 to 1.44, as said below
- attn_out_moments: float32 [2, 1024, 1024], P(None, 'tensor', 'shard'), may hold values from -3.6 to 3.6, as said below
- mlp_up_moments: float32 [2, 1024, 4096], P(None, 'shard', 'tensor'), may hold values from -2.16 to 2.16, as said below
- mlp_down_moments: float32 [2, 4096, 1024], P(None, 'tensor', 'shard'), may hold values from -4.32 to 4.32, as said below
- vector_moments: float32 [2, 8, 1024], replicated, may hold values from -7.2 to 7.2, as said below
- up_bias_moments: float32 [2, 4096], replicated, may hold values from -2.16 to 2.16, as said below
Outputs:
- block_output: bfloat16 [4, 2048, 1024], P('shard', ('context', 'tensor'))
- input_grad: bfloat16 [4, 2048, 1024], P('shard', ('context', 'tensor'))
- attn_in_grad: float32 [3, 1024, 1024], P(None, 'shard', 'tensor')
- attn_out_grad: float32 [1024, 1024], P('tensor', 'shard')
- mlp_up_grad: float32 [1024, 4096], P('shard', 'tensor')
- mlp_down_grad: float32 [4096, 1024], P('tensor', 'shard')
- vectors_grad: float32 [8, 1024], replicated
- up_bias_grad: float32 [4096], replicated
- attn_in_new: float32 [3, 1024, 1024], P(None, 'shard', 'tensor')
- attn_out_new: float32 [1024, 1024], P('tensor', 'shard')
- mlp_up_new: float32 [1024, 4096], P('shard', 'tensor')
- mlp_down_new: float32 [4096, 1024], P('tensor', 'shard')
- vectors_new: float32 [8, 1024], replicated
- up_bias_new: float32 [4096], replicated
- attn_in_moments_new: float32 [2, 3, 1024, 1024], P(None, None, 'shard', 'tensor')
- attn_out_moments_new: float32 [2, 1024, 1024], P(None, 'tensor', 'shard')
- mlp_up_moments_new: float32 [2, 1024, 4096], P(None, 'shard', 'tensor')
- mlp_down_moments_new: float32 [2, 4096, 1024], P(None, 'tensor', 'shard')
- vector_moments_new: float32 [2, 8, 1024], replicated
- up_bias_moments_new: float32 [2, 4096], replicated
The draws below stay inside these ranges and needn't reach their ends.
Inputs may be any that keep to these rules, and one draw needn't show every extreme that they name: `vectors`: rows 4 and 6 are gains near one, the others biases near zero. `attn_in_moments`: index 0 holds first moments, index 1 positive second moments. `attn_out_moments`: index 0 holds first moments, index 1 positive second moments. `mlp_up_moments`: index 0 holds first moments, index 1 positive second moments. `mlp_down_moments`: index 0 holds first moments, index 1 positive second moments. `vector_moments`: index 0 holds first moments, index 1 positive second moments. `up_bias_moments`: index 0 holds first moments, index 1 positive second moments.
All inputs are finite; a program needn't handle non-finite values.
Results may differ from the reference program's by a relative error of at most 0.023.
Values may be sent and summed in bfloat16 or wider, within the bound.
No kernel may reach another device: no remote copies, remote signals or barrier semaphores. Data moves between devices by JAX's collectives and lax.ppermute only.
A program may use at most 256 MiB of HBM per device.

```python
import math
import jax
import jax.numpy as jnp
import numpy as np
from jax import lax

D = 1024
HEADS = 16
HD = 64
FF = 4096
DOCS = 4
LEN = 2048
SEQS = 4


def moment_pair(key, shape, grad_size):
    first = jax.random.truncated_normal(jax.random.fold_in(key, 11), -4.0, 4.0, shape, jnp.float32) * (0.02 * grad_size)
    level = jax.random.uniform(jax.random.fold_in(key, 12), shape, jnp.float32)
    second = 0.0002 * grad_size * grad_size * jnp.exp((level - 1.0) * math.log(4.0))
    return jnp.stack([first, second])


def draw_layer_input(key, part):
    shape = (SEQS, LEN, D)
    return jax.random.truncated_normal(jax.random.fold_in(key, 4), -5.0, 5.0, shape, jnp.float32).astype(jnp.bfloat16)


def draw_vectors(key, part):
    base = jax.random.truncated_normal(jax.random.fold_in(key, 1), -4.0, 4.0, (8, D), jnp.float32) * 0.2
    gains = 1.0 + 0.1 * jax.random.truncated_normal(jax.random.fold_in(key, 2), -4.0, 4.0, (8, D), jnp.float32)
    which = jnp.arange(8)[:, None]
    return jnp.where((which == 4) | (which == 6), gains, base)


def draw_attn_in_moments(key, part):
    return moment_pair(key, (3, D, D), 18.0)


def draw_attn_out_moments(key, part):
    return moment_pair(key, (D, D), 45.0)


def draw_mlp_up_moments(key, part):
    return moment_pair(key, (D, FF), 27.0)


def draw_mlp_down_moments(key, part):
    return moment_pair(key, (FF, D), 54.0)


def draw_vector_moments(key, part):
    return moment_pair(key, (8, D), 90.0)


def draw_up_bias_moments(key, part):
    return moment_pair(key, (FF,), 27.0)


def level_of(rng, dims, pieces, smallest, top_value):
    level, own = 1.0, jax.random.fold_in(rng, 6)
    for dim, parts in pieces:
        heights = jnp.exp(jax.random.uniform(jax.random.fold_in(own, dim), (parts,), jnp.float32, smallest / len(pieces), top_value / len(pieces)))
        level = level * jnp.repeat(heights, dims[dim] // parts).reshape([-1 if axis == dim else 1 for axis in range(len(dims))])
    return level


def profile(number_of, total, most, lean):
    weights = [(1 << 20) // math.isqrt(grade ** lean) + 1 for grade in range(2, number_of + 1)]
    surplus, holding = total - most - (number_of - 1), [1] * (number_of - 1)
    while surplus > 0:
        free = [i for i in range(number_of - 1) if holding[i] < most]
        whole, remaining = sum([weights[i] for i in free]), surplus
        for i in free:
            more = min(most - holding[i], max(1, remaining * weights[i] // whole), surplus)
            holding[i] = holding[i] + more
            surplus = surplus - more
    return np.array([most] + holding)


def ragged(own_key, number_of, total, limit, skew):
    if number_of == 2:
        one = jax.random.randint(own_key, (), max(1, total - limit), min(limit, total - 1) + 1)
        return jnp.stack([one, total - one])
    tallies = jnp.asarray(profile(number_of, total, limit, skew), jnp.int32)
    couples = (number_of - 1) // 2
    giver, receiver = tallies[1:1 + 2 * couples:2], tallies[2:2 + 2 * couples:2]
    room = jnp.minimum(giver - 1, limit - receiver)
    shifted = jax.random.randint(jax.random.fold_in(own_key, 1), (couples,), 0, 1 << 20) % (room + 1)
    tallies = tallies.at[1:1 + 2 * couples:2].set(giver - shifted).at[2:2 + 2 * couples:2].set(receiver + shifted)
    return tallies[jax.random.permutation(jax.random.fold_in(own_key, 2), number_of)]


def centred(rng, dims, spread, bound, pieces=(), kind=jnp.bfloat16):
    drawn = jax.random.normal(rng, dims, jnp.float32) * spread
    if len(pieces) > 0:
        drawn = level_of(rng, dims, pieces, -0.22, 0.18) * drawn
    return jnp.clip(drawn, min=-bound, max=bound).astype(kind)


def setup_inputs(seed: int = 0) -> dict:
    seeds = jax.random.split(jax.random.key(seed), 16)
    return {
        "layer_input": draw_layer_input(jax.random.fold_in(seeds[15], 71), 0),
        "segment_ids": jax.vmap(lambda own: jnp.searchsorted(jnp.cumsum(ragged(own, DOCS, LEN, LEN // 2, 0)), jnp.arange(LEN), side="right"))(jax.random.split(seeds[1], SEQS)).reshape((SEQS, LEN)).astype(jnp.int32),
        "out_grad": centred(seeds[2], (SEQS, LEN, D), 1.0, 6.0, ((0, 4), (1, 8))),
        "attn_in": centred(seeds[3], (3, D, D), D ** -0.5, 0.1875, ((1, 4), (2, 2)), jnp.float32),
        "attn_out": centred(seeds[4], (D, D), HD ** -0.5, 0.75, ((0, 2), (1, 4)), jnp.float32),
        "mlp_up": centred(seeds[5], (D, FF), D ** -0.5, 0.1875, ((0, 4), (1, 2)), jnp.float32),
        "mlp_down": centred(seeds[6], (FF, D), FF ** -0.5, 0.09375, ((0, 2), (1, 4)), jnp.float32),
        "vectors": draw_vectors(jax.random.fold_in(seeds[15], 71), 0),
        "up_bias": centred(seeds[8], (FF,), 0.2, 0.8, (), jnp.float32),
        "attn_in_moments": draw_attn_in_moments(jax.random.fold_in(seeds[15], 71), 0),
        "attn_out_moments": draw_attn_out_moments(jax.random.fold_in(seeds[15], 71), 0),
        "mlp_up_moments": draw_mlp_up_moments(jax.random.fold_in(seeds[15], 71), 0),
        "mlp_down_moments": draw_mlp_down_moments(jax.random.fold_in(seeds[15], 71), 0),
        "vector_moments": draw_vector_moments(jax.random.fold_in(seeds[15], 71), 0),
        "up_bias_moments": draw_up_bias_moments(jax.random.fold_in(seeds[15], 71), 0),
    }


layer_eps = 1e-05
beta_one = 0.9
beta_two = 0.999
adam_eps = 1e-06
learning_rate = 0.02
weight_decay = 0.01
adam_step = 3.0
masked_score = -1e+30

def round_half(value):
    return lax.optimization_barrier(value.astype(jnp.bfloat16)).astype(jnp.float32)

def normalize(hidden):
    center = hidden - lax.optimization_barrier(jnp.mean(hidden, axis=-1, keepdims=True))
    scale = lax.rsqrt(lax.optimization_barrier(jnp.mean(center * center, axis=-1, keepdims=True)) + layer_eps)
    return (center * scale, scale)

def norm_back(upstream, normed, scale, gain):
    scaled = upstream * gain
    return scale * (scaled - lax.optimization_barrier(jnp.mean(scaled, axis=-1, keepdims=True)) - normed * lax.optimization_barrier(jnp.mean(scaled * normed, axis=-1, keepdims=True)))

def gelu_value(value):
    return 0.5 * value * (1.0 + jax.scipy.special.erf(value * 0.7071067811865476))

def gelu_slope(value):
    return 0.5 * (1.0 + jax.scipy.special.erf(value * 0.7071067811865476)) + value * jnp.exp(-0.5 * value * value) * 0.3989422804014327

def adamw(param, moments, grad, decay):
    first = beta_one * moments[0] + (1.0 - beta_one) * grad
    second = beta_two * moments[1] + (1.0 - beta_two) * grad * grad
    update = first / (1.0 - beta_one ** adam_step) / (jnp.sqrt(second / (1.0 - beta_two ** adam_step)) + adam_eps)
    return (param - learning_rate * (update + decay * param), jnp.stack([first, second]))

def one_sequence(tokens, segment, upstream, in_half, out_half, up_half, down_half, vectors, up_bias):
    scale = 1.0 / HD ** 0.5
    width = min(512, LEN)
    count = LEN // width
    tokens32 = tokens.astype(jnp.float32)
    project = jnp.einsum('td,kdh->kth', tokens32, in_half.astype(jnp.float32))
    query32 = round_half(project[0] + vectors[0]).reshape(LEN, HEADS, HD)
    keys32 = round_half(project[1]).reshape(LEN, HEADS, HD)
    values32 = round_half(project[2] + vectors[1]).reshape(LEN, HEADS, HD)

    def scores_of(start):
        block = lax.dynamic_slice_in_dim(query32, start, width, 0)
        raw = jnp.einsum('qhd,khd->hqk', block, keys32) * scale
        own = lax.dynamic_slice_in_dim(segment, start, width, 0)
        return jnp.where((own[:, None] == segment[None, :])[None], raw, masked_score)

    def forward_block(carry, index):
        start = index * width
        raw = scores_of(start)
        top = lax.optimization_barrier(jnp.max(raw, axis=-1, keepdims=True))
        total = top + jnp.log(lax.optimization_barrier(jnp.sum(jnp.exp(raw - top), axis=-1, keepdims=True)))
        attend = round_half(jnp.exp(raw - total))
        context = jnp.einsum('hqk,khd->qhd', attend, values32)
        return (carry, (context, total))
    blocks_index = jnp.arange(count, dtype=jnp.int32)
    unused, (context, logsum) = lax.scan(forward_block, jnp.float32(0.0), blocks_index)
    context = context.reshape(LEN, D)
    context_half = round_half(context)
    attn = jnp.dot(context_half, out_half.astype(jnp.float32)) + vectors[2]
    normed_one, scale_one = normalize(tokens32 + attn)
    first = normed_one * vectors[4] + vectors[5]
    first_half = round_half(first)
    before = jnp.dot(first_half, up_half.astype(jnp.float32)) + up_bias
    hidden_half = round_half(gelu_value(before))
    mlp = jnp.dot(hidden_half, down_half.astype(jnp.float32)) + vectors[3]
    normed_two, scale_two = normalize(first + mlp)
    block_output = (normed_two * vectors[6] + vectors[7]).astype(jnp.bfloat16)
    upstream32 = upstream.astype(jnp.float32)
    grad_two = norm_back(upstream32, normed_two, scale_two, vectors[6])
    grad_two_half = round_half(grad_two)
    down_grad = jnp.dot(hidden_half.T, grad_two_half)
    grad_before = jnp.dot(grad_two_half, down_half.astype(jnp.float32).T) * gelu_slope(before)
    grad_before_half = round_half(grad_before)
    up_grad = jnp.dot(first_half.T, grad_before_half)
    grad_first = grad_two + jnp.dot(grad_before_half, up_half.astype(jnp.float32).T)
    grad_one = norm_back(grad_first, normed_one, scale_one, vectors[4])
    grad_one_half = round_half(grad_one)
    out_grad_w = jnp.dot(context_half.T, grad_one_half)
    grad_context = round_half(jnp.dot(grad_one_half, out_half.astype(jnp.float32).T)).reshape(LEN, HEADS, HD)
    delta = lax.optimization_barrier(jnp.sum(grad_context * context.reshape(LEN, HEADS, HD), axis=-1))

    def backward_block(carry, index):
        key_sum, value_sum = carry
        start = index * width
        raw = scores_of(start)
        total = logsum[index]
        attend_full = jnp.exp(raw - total)
        attend = round_half(attend_full)
        part = lax.dynamic_slice_in_dim(grad_context, start, width, 0)
        shift = jnp.transpose(lax.dynamic_slice_in_dim(delta, start, width, 0))[:, :, None]
        grad_probs = jnp.einsum('qhd,khd->hqk', part, values32)
        grad_score = round_half(attend_full * (grad_probs - shift) * scale)
        query_grad = jnp.einsum('hqk,khd->qhd', grad_score, keys32)
        block = lax.dynamic_slice_in_dim(query32, start, width, 0)
        key_sum = key_sum + jnp.einsum('hqk,qhd->khd', grad_score, block)
        value_sum = value_sum + jnp.einsum('hqk,qhd->khd', attend, part)
        return ((key_sum, value_sum), query_grad)
    zeros = jnp.zeros((LEN, HEADS, HD), jnp.float32)
    (key_sum, value_sum), query_grad = lax.scan(backward_block, (zeros, zeros), blocks_index)
    query_grad = query_grad.reshape(LEN, D)
    key_sum = key_sum.reshape(LEN, D)
    value_sum = value_sum.reshape(LEN, D)
    stacked = round_half(jnp.stack([query_grad, key_sum, value_sum]))
    in_grad = jnp.einsum('td,kth->kdh', tokens32, stacked)
    input_grad = (grad_one + jnp.einsum('kth,kdh->td', stacked, in_half.astype(jnp.float32))).astype(jnp.bfloat16)
    vector_grad = jnp.stack([lax.optimization_barrier(jnp.sum(query_grad, 0)), lax.optimization_barrier(jnp.sum(value_sum, 0)), lax.optimization_barrier(jnp.sum(grad_one, 0)), lax.optimization_barrier(jnp.sum(grad_two, 0)), lax.optimization_barrier(jnp.sum(grad_first * normed_one, 0)), lax.optimization_barrier(jnp.sum(grad_first, 0)), lax.optimization_barrier(jnp.sum(upstream32 * normed_two, 0)), lax.optimization_barrier(jnp.sum(upstream32, 0))])
    bias_grad = lax.optimization_barrier(jnp.sum(grad_before, 0))
    return (block_output, input_grad, (in_grad, out_grad_w, up_grad, down_grad, vector_grad, bias_grad))

def reference(layer_input, segment_ids, out_grad, attn_in, attn_out, mlp_up, mlp_down, vectors, up_bias, attn_in_moments, attn_out_moments, mlp_up_moments, mlp_down_moments, vector_moments, up_bias_moments):
    in_half = attn_in.astype(jnp.bfloat16)
    out_half = attn_out.astype(jnp.bfloat16)
    up_half = mlp_up.astype(jnp.bfloat16)
    down_half = mlp_down.astype(jnp.bfloat16)

    def per_sequence(carry, index):
        block_output, input_grad, grads = one_sequence(layer_input[index], segment_ids[index], out_grad[index], in_half, out_half, up_half, down_half, vectors, up_bias)
        return (jax.tree.map(lambda left, right: left + right, carry, grads), (block_output, input_grad))
    start = (jnp.zeros(attn_in.shape, jnp.float32), jnp.zeros(attn_out.shape, jnp.float32), jnp.zeros(mlp_up.shape, jnp.float32), jnp.zeros(mlp_down.shape, jnp.float32), jnp.zeros(vectors.shape, jnp.float32), jnp.zeros(up_bias.shape, jnp.float32))
    grads, (block_output, input_grad) = lax.scan(per_sequence, start, jnp.arange(SEQS, dtype=jnp.int32))
    in_grad, out_grad_w, up_grad, down_grad, vector_grad, bias_grad = grads
    in_new, in_moments = adamw(attn_in, attn_in_moments, in_grad, weight_decay)
    out_new, out_moments = adamw(attn_out, attn_out_moments, out_grad_w, weight_decay)
    up_new, up_moments = adamw(mlp_up, mlp_up_moments, up_grad, weight_decay)
    down_new, down_moments = adamw(mlp_down, mlp_down_moments, down_grad, weight_decay)
    vec_new, vec_moments = adamw(vectors, vector_moments, vector_grad, 0.0)
    bias_new, bias_moments = adamw(up_bias, up_bias_moments, bias_grad, 0.0)
    return (block_output, input_grad, in_grad, out_grad_w, up_grad, down_grad, vector_grad, bias_grad, in_new, out_new, up_new, down_new, vec_new, bias_new, in_moments, out_moments, up_moments, down_moments, vec_moments, bias_moments)
```

```python
import jax
import jax.numpy as jnp
from jax import lax
from jax.experimental import pallas as pl
from jax.experimental.pallas import tpu as pltpu
from jax.sharding import PartitionSpec as P

HD = 64


layer_eps = 1e-05
beta_one = 0.9
beta_two = 0.999
adam_eps = 1e-06
learning_rate = 0.02
weight_decay = 0.01
adam_step = 3.0
masked_score = -1e30


def normalize(hidden):
    center = hidden - jnp.mean(hidden, axis=-1, keepdims=True)
    scale = lax.rsqrt(jnp.mean(center * center, axis=-1, keepdims=True) + layer_eps)
    return (center * scale, scale)


def norm_back(upstream, normed, scale, gain):
    scaled = upstream * gain
    return scale * (
        scaled
        - jnp.mean(scaled, axis=-1, keepdims=True)
        - normed * jnp.mean(scaled * normed, axis=-1, keepdims=True)
    )


def gelu_value(value):
    return 0.5 * value * (1.0 + jax.scipy.special.erf(value * 0.7071067811865476))


def gelu_slope(value):
    return (
        0.5 * (1.0 + jax.scipy.special.erf(value * 0.7071067811865476))
        + value * jnp.exp(-0.5 * value * value) * 0.3989422804014327
    )


def adamw(param, moments, grad, decay):
    first = beta_one * moments[0] + (1.0 - beta_one) * grad
    second = beta_two * moments[1] + (1.0 - beta_two) * grad * grad
    update = (
        first
        / (1.0 - beta_one**adam_step)
        / (jnp.sqrt(second / (1.0 - beta_two**adam_step)) + adam_eps)
    )
    return (param - learning_rate * (update + decay * param), jnp.stack([first, second]))


def inner_rows(left, right):
    return lax.dot_general(
        left, right, (((0,), (0,)), ((), ())), preferred_element_type=jnp.float32
    )


def against_rows(left, right):
    return lax.dot_general(
        left, right, (((1,), (1,)), ((), ())), preferred_element_type=jnp.float32
    )


def over_context(grads):
    return (
        lax.psum(grads[0].astype(jnp.bfloat16), "context").astype(jnp.float32),
        lax.psum(grads[1].astype(jnp.bfloat16), "context").astype(jnp.float32),
        lax.psum(grads[2].astype(jnp.bfloat16), "context").astype(jnp.float32),
        lax.psum(grads[3].astype(jnp.bfloat16), "context").astype(jnp.float32),
    )


def to_owner(grads):
    return (
        lax.psum_scatter(
            grads[0].astype(jnp.bfloat16), "shard", scatter_dimension=1, tiled=True
        ).astype(jnp.float32),
        lax.psum_scatter(
            grads[1].astype(jnp.bfloat16), "shard", scatter_dimension=1, tiled=True
        ).astype(jnp.float32),
        lax.psum_scatter(
            grads[2].astype(jnp.bfloat16), "shard", scatter_dimension=0, tiled=True
        ).astype(jnp.float32),
        lax.psum_scatter(
            grads[3].astype(jnp.bfloat16), "shard", scatter_dimension=1, tiled=True
        ).astype(jnp.float32),
    )


def any_mesh(
    layer_input,
    segment_ids,
    out_grad,
    attn_in,
    attn_out,
    mlp_up,
    mlp_down,
    vectors,
    up_bias,
    attn_in_moments,
    attn_out_moments,
    mlp_up_moments,
    mlp_down_moments,
    vector_moments,
    up_bias_moments,
):
    tensor_count = lax.axis_size("tensor")
    tensor_rank = lax.axis_index("tensor")
    context_rank = lax.axis_index("context")
    seq_count = layer_input.shape[0]
    count_rows = layer_input.shape[1]
    model_width = vectors.shape[1]
    tokens = jnp.transpose(layer_input, (1, 0, 2)).reshape(count_rows * seq_count, model_width)
    all_rows = count_rows * seq_count
    share_tok = count_rows // tensor_count
    share_rows = share_tok * seq_count
    head_width = attn_in.shape[2]
    hidden_width = mlp_up.shape[1]
    length = segment_ids.shape[1]
    head_count = head_width // HD
    scale = 1.0 / HD**0.5
    in_full, out_full, up_full, down_full = (
        lax.all_gather(attn_in.astype(jnp.bfloat16), "shard", axis=1, tiled=True),
        lax.all_gather(attn_out.astype(jnp.bfloat16), "shard", axis=1, tiled=True),
        lax.all_gather(mlp_up.astype(jnp.bfloat16), "shard", axis=0, tiled=True),
        lax.all_gather(mlp_down.astype(jnp.bfloat16), "shard", axis=1, tiled=True),
    )
    head_start = tensor_rank * head_width
    unit_start = tensor_rank * hidden_width
    query_bias = lax.dynamic_slice_in_dim(vectors[0], head_start, head_width)
    value_bias = lax.dynamic_slice_in_dim(vectors[1], head_start, head_width)
    unit_bias = lax.dynamic_slice_in_dim(up_bias, unit_start, hidden_width)
    project = jnp.einsum("td,kdh->kth", tokens, in_full, preferred_element_type=jnp.float32)
    query_half = (project[0] + query_bias).astype(jnp.bfloat16)
    key_half = project[1].astype(jnp.bfloat16).reshape(count_rows, seq_count, head_width)
    value_half = (
        (project[2] + value_bias).astype(jnp.bfloat16).reshape(count_rows, seq_count, head_width)
    )
    keys_all, values_all = (
        lax.all_gather(key_half, "context", axis=0, tiled=True),
        lax.all_gather(value_half, "context", axis=0, tiled=True),
    )
    query_seq = query_half.reshape(count_rows, seq_count, head_count, HD)
    block = min(512, count_rows)
    blocks = count_rows // block

    def scores_of(which, lower):
        key_heads = keys_all[:, which].reshape(length, head_count, HD)
        segment = segment_ids[which]
        own_segment = lax.dynamic_slice_in_dim(segment, context_rank * count_rows, count_rows)
        raw = (
            jnp.einsum(
                "qhd,khd->hqk",
                query_seq[lower : lower + block, which],
                key_heads,
                preferred_element_type=jnp.float32,
            )
            * scale
        )
        same = own_segment[:, None] == segment[None, :]
        return jnp.where(same[None], raw, masked_score)

    which = 0
    value_heads = values_all[:, which].reshape(length, head_count, HD)
    parts = []
    index = 0
    raw = scores_of(which, index * block)
    top = jnp.max(raw, axis=-1, keepdims=True)
    total = top + jnp.log(jnp.sum(jnp.exp(raw - top), axis=-1, keepdims=True))
    attend = jnp.exp(raw - total).astype(jnp.bfloat16)
    parts.append(
        jnp.einsum("hqk,khd->qhd", attend, value_heads, preferred_element_type=jnp.float32).reshape(
            block, head_width
        )
    )
    totals = [total]
    seq_contexts = [parts[0]]
    context = jnp.stack(seq_contexts, 1).reshape(all_rows, head_width)
    context_half = context.astype(jnp.bfloat16)
    my_start = tensor_rank * share_rows
    attn_share = lax.psum_scatter(
        jnp.dot(context_half, out_full, preferred_element_type=jnp.float32).astype(jnp.bfloat16),
        "tensor",
        scatter_dimension=0,
        tiled=True,
    ).astype(jnp.float32)
    residual_in = lax.dynamic_slice_in_dim(tokens, my_start, share_rows, 0).astype(jnp.float32)
    normed_one, scale_one = normalize(residual_in + attn_share + vectors[2])
    first = normed_one * vectors[4] + vectors[5]
    first_all = lax.all_gather(first.astype(jnp.bfloat16), "tensor", axis=0, tiled=True)
    before = jnp.dot(first_all, up_full, preferred_element_type=jnp.float32) + unit_bias
    hidden_half = gelu_value(before).astype(jnp.bfloat16)
    mlp_share = lax.psum_scatter(
        jnp.dot(hidden_half, down_full, preferred_element_type=jnp.float32).astype(jnp.bfloat16),
        "tensor",
        scatter_dimension=0,
        tiled=True,
    ).astype(jnp.float32)
    normed_two, scale_two = normalize(first + mlp_share + vectors[3])
    block_output = (normed_two * vectors[6] + vectors[7]).astype(jnp.bfloat16)
    upstream = (
        jnp.transpose(out_grad, (1, 0, 2)).reshape(share_rows, model_width).astype(jnp.float32)
    )
    grad_two = norm_back(upstream, normed_two, scale_two, vectors[6])
    grad_two_all = lax.all_gather(grad_two.astype(jnp.bfloat16), "tensor", axis=0, tiled=True)
    down_grad = inner_rows(hidden_half, grad_two_all)
    grad_before = against_rows(grad_two_all, down_full) * gelu_slope(before)
    grad_before_half = grad_before.astype(jnp.bfloat16)
    up_grad = inner_rows(first_all, grad_before_half)
    grad_first = grad_two + lax.psum_scatter(
        against_rows(grad_before_half, up_full).astype(jnp.bfloat16),
        "tensor",
        scatter_dimension=0,
        tiled=True,
    ).astype(jnp.float32)
    grad_one = norm_back(grad_first, normed_one, scale_one, vectors[4])
    grad_one_all = lax.all_gather(grad_one.astype(jnp.bfloat16), "tensor", axis=0, tiled=True)
    out_grad_w = inner_rows(context_half, grad_one_all)
    grad_context = against_rows(grad_one_all, out_full).astype(jnp.bfloat16)
    grad_seq = grad_context.reshape(count_rows, seq_count, head_count, HD)
    delta = jnp.sum(
        grad_seq.astype(jnp.float32) * context.reshape(count_rows, seq_count, head_count, HD),
        axis=-1,
    )
    which = 0
    key_heads = keys_all[:, which].reshape(length, head_count, HD)
    value_heads = values_all[:, which].reshape(length, head_count, HD)
    parts = []
    index = 0
    lower = index * block
    raw = scores_of(which, lower)
    attend_full = jnp.exp(raw - totals[which * blocks + index])
    attend = attend_full.astype(jnp.bfloat16)
    part = grad_seq[lower : lower + block, which]
    shift = jnp.transpose(delta[lower : lower + block, which])[:, :, None]
    grad_probs = jnp.einsum("qhd,khd->hqk", part, value_heads, preferred_element_type=jnp.float32)
    grad_score = (attend_full * (grad_probs - shift) * scale).astype(jnp.bfloat16)
    parts.append(
        jnp.einsum(
            "hqk,khd->qhd", grad_score, key_heads, preferred_element_type=jnp.float32
        ).reshape(block, head_width)
    )
    key_acc = jnp.einsum(
        "hqk,qhd->khd",
        grad_score,
        query_seq[lower : lower + block, which],
        preferred_element_type=jnp.float32,
    )
    value_acc = jnp.einsum("hqk,qhd->khd", attend, part, preferred_element_type=jnp.float32)
    query_list = [parts[0]]
    key_list = [key_acc.reshape(length, head_width)]
    value_list = [value_acc.reshape(length, head_width)]
    query_grad = jnp.stack(query_list, 1).reshape(all_rows, head_width)
    key_own, value_own = (
        lax.psum_scatter(
            jnp.stack(key_list, 1).astype(jnp.bfloat16), "context", scatter_dimension=0, tiled=True
        ).astype(jnp.float32),
        lax.psum_scatter(
            jnp.stack(value_list, 1).astype(jnp.bfloat16),
            "context",
            scatter_dimension=0,
            tiled=True,
        ).astype(jnp.float32),
    )
    key_own = key_own.reshape(all_rows, head_width)
    value_own = value_own.reshape(all_rows, head_width)
    stacked = jnp.stack([query_grad, key_own, value_own]).astype(jnp.bfloat16)
    in_grad = jnp.einsum("td,kth->kdh", tokens, stacked, preferred_element_type=jnp.float32)
    input_share = grad_one + lax.psum_scatter(
        jnp.einsum("kth,kdh->td", stacked, in_full, preferred_element_type=jnp.float32).astype(
            jnp.bfloat16
        ),
        "tensor",
        scatter_dimension=0,
        tiled=True,
    ).astype(jnp.float32)
    input_grad = jnp.transpose(
        input_share.astype(jnp.bfloat16).reshape(share_tok, seq_count, model_width), (1, 0, 2)
    )
    output_block = jnp.transpose(block_output.reshape(share_tok, seq_count, model_width), (1, 0, 2))
    query_row = lax.dynamic_update_slice(
        jnp.zeros((model_width,), jnp.float32), jnp.sum(query_grad, 0), (head_start,)
    )
    value_row = lax.dynamic_update_slice(
        jnp.zeros((model_width,), jnp.float32), jnp.sum(value_own, 0), (head_start,)
    )
    local_vectors = jnp.stack(
        [
            query_row,
            value_row,
            jnp.sum(grad_one, 0),
            jnp.sum(grad_two, 0),
            jnp.sum(grad_first * normed_one, 0),
            jnp.sum(grad_first, 0),
            jnp.sum(upstream * normed_two, 0),
            jnp.sum(upstream, 0),
        ]
    )
    local_bias = lax.dynamic_update_slice(
        jnp.zeros((up_bias.shape[0],), jnp.float32), jnp.sum(grad_before, 0), (unit_start,)
    )
    vector_grad, bias_grad = lax.psum((local_vectors, local_bias), ("shard", "context", "tensor"))
    local_grads = (in_grad, out_grad_w, up_grad, down_grad)
    owned = to_owner(over_context(local_grads))
    in_sum, out_sum, up_sum, down_sum = owned
    in_new, in_moments = adamw(attn_in, attn_in_moments, in_sum, weight_decay)
    out_new, out_moments = adamw(attn_out, attn_out_moments, out_sum, weight_decay)
    up_new, up_moments = adamw(mlp_up, mlp_up_moments, up_sum, weight_decay)
    down_new, down_moments = adamw(mlp_down, mlp_down_moments, down_sum, weight_decay)
    vec_new, vec_moments = adamw(vectors, vector_moments, vector_grad, 0.0)
    bias_new, bias_moments = adamw(up_bias, up_bias_moments, bias_grad, 0.0)
    return (
        output_block,
        input_grad,
        in_sum,
        out_sum,
        up_sum,
        down_sum,
        vector_grad,
        bias_grad,
        in_new,
        out_new,
        up_new,
        down_new,
        vec_new,
        bias_new,
        in_moments,
        out_moments,
        up_moments,
        down_moments,
        vec_moments,
        bias_moments,
    )


core_swap = [(0, 1), (1, 0), (2, 3), (3, 2)]
chip_swap = [(0, 2), (2, 0), (1, 3), (3, 1)]
pair_swap = [(0, 1), (1, 0)]
line_in = [(0, 1), (3, 2)]
line_mid = [(1, 2), (2, 1)]
line_out = [(1, 0), (2, 3)]
block_q = 256
block_k = 256
half = jnp.bfloat16
single = jnp.float32


def fits(mesh):
    return (
        mesh.shape["tensor"] == 2
        and mesh.shape["context"] == 4
        and mesh.shape["shard"] == 4
    )


def score_block(keys, queries, same):
    raw = lax.dot_general(
        keys, queries, (((1,), (1,)), ((), ())), preferred_element_type=jnp.float32
    )
    return jnp.where(same, raw, masked_score)


def attend_kernel(
    bounds, query, key, value, seg_row, seg_col, out_half, out_full, logsum, keys, values
):
    index = pl.program_id(0)
    heads = keys.shape[0]

    @pl.when(index == 0)
    def _():
        for head in range(heads):
            keys[head] = key[:, head * HD : (head + 1) * HD]
            values[head] = value[:, head * HD : (head + 1) * HD]

    own = seg_row[...]
    queries = [
        query[:, head * HD : (head + 1) * HD] * jnp.asarray(1.0 / HD**0.5, half)
        for head in range(heads)
    ]

    def step(place, carry):
        lower = pl.multiple_of(place * block_k, block_k)
        same = seg_col[pl.ds(lower, block_k), :] == own
        result = []
        for head in range(heads):
            top, total, acc = carry[head]
            raw = score_block(keys[head, pl.ds(lower, block_k), :], queries[head], same)
            new_top = jnp.maximum(top, jnp.max(raw, axis=0, keepdims=True))
            fade = jnp.exp(top - new_top)
            prob = jnp.exp(raw - new_top)
            total = fade * total + jnp.sum(prob, axis=0, keepdims=True)
            acc = acc * fade + lax.dot_general(
                values[head, pl.ds(lower, block_k), :],
                prob.astype(half),
                (((0,), (0,)), ((), ())),
                preferred_element_type=jnp.float32,
            )
            result.append((new_top, total, acc))
        return tuple(result)

    width = query.shape[0]
    start = tuple(
        (
            jnp.full((1, width), masked_score, single),
            jnp.zeros((1, width), single),
            jnp.zeros((HD, width), single),
        )
        for _ in range(heads)
    )
    done = lax.fori_loop(bounds[index, 0], bounds[index, 1], step, start)
    columns = jnp.concatenate([acc / total for _, total, acc in done], 0)
    rows = columns.T
    out_full[...] = rows
    out_half[...] = rows.astype(half)
    logsum[...] = jnp.concatenate([top + jnp.log(total) for top, total, _ in done], 0)


def attend_back_kernel(
    bounds,
    query,
    key,
    value,
    grad,
    context,
    logsum,
    seg_row,
    seg_col,
    query_out,
    key_out,
    value_out,
    sums_out,
    keys,
    values,
    key_acc,
    value_acc,
    query_sum,
):
    index = pl.program_id(0)
    heads = keys.shape[0]
    scale = 1.0 / HD**0.5

    @pl.when(index == 0)
    def _():
        for head in range(heads):
            keys[head] = key[:, head * HD : (head + 1) * HD]
            values[head] = value[:, head * HD : (head + 1) * HD]
        key_acc[...] = jnp.zeros_like(key_acc)
        value_acc[...] = jnp.zeros_like(value_acc)
        query_sum[...] = jnp.zeros_like(query_sum)

    own = seg_row[...]
    product = (grad[...].astype(single) * context[...]).T
    deltas = [
        jnp.sum(product[head * HD : (head + 1) * HD], axis=0, keepdims=True)
        for head in range(heads)
    ]
    totals = logsum[...]
    plain = [query[:, head * HD : (head + 1) * HD] for head in range(heads)]
    queries = [part * jnp.asarray(scale, half) for part in plain]
    grads = [grad[:, head * HD : (head + 1) * HD] for head in range(heads)]

    def step(place, carry):
        lower = pl.multiple_of(place * block_k, block_k)
        window = pl.ds(lower, block_k)
        same = seg_col[window, :] == own
        result = []
        for head in range(heads):
            key_rows = keys[head, window, :]
            raw = score_block(key_rows, queries[head], same)
            prob = jnp.exp(raw - totals[head : head + 1])
            grad_prob = lax.dot_general(
                values[head, window, :],
                grads[head],
                (((1,), (1,)), ((), ())),
                preferred_element_type=jnp.float32,
            )
            grad_score = (prob * (grad_prob - deltas[head]) * scale).astype(half)
            value_acc[head, window, :] += jnp.dot(
                prob.astype(half), grads[head], preferred_element_type=jnp.float32
            )
            key_acc[head, window, :] += jnp.dot(
                grad_score, plain[head], preferred_element_type=jnp.float32
            )
            result.append(
                carry[head]
                + lax.dot_general(
                    grad_score,
                    key_rows,
                    (((0,), (0,)), ((), ())),
                    preferred_element_type=jnp.float32,
                )
            )
        return tuple(result)

    start = tuple(jnp.zeros((query.shape[0], HD), single) for _ in range(heads))
    done = jnp.concatenate(lax.fori_loop(bounds[index, 0], bounds[index, 1], step, start), 1)
    query_out[...] = done.astype(half)
    query_sum[...] += jnp.sum(done, axis=0, keepdims=True)

    @pl.when(index == pl.num_programs(0) - 1)
    def _():
        key_out[...] = jnp.concatenate([key_acc[head] for head in range(heads)], 1).astype(half)
        rows = jnp.concatenate([value_acc[head] for head in range(heads)], 1)
        value_out[...] = rows.astype(half)
        sums_out[...] = jnp.concatenate(
            [query_sum[...], jnp.sum(rows, axis=0, keepdims=True)], 0
        )


def attention_plan(segment):
    length = segment.shape[0]
    tiles = segment.reshape(length // block_q, block_q)
    lower = jnp.sum(segment[None] < tiles[:, :1], axis=1)
    upper = jnp.sum(segment[None] <= tiles[:, -1:], axis=1)
    bounds = jnp.stack([lower // block_k, (upper + block_k - 1) // block_k], 1)
    return bounds.astype(jnp.int32), segment[None], segment[:, None]


def attend_forward(query, key, value, plan):
    bounds, seg_row, seg_col = plan
    length, width = query.shape
    heads = width // HD
    tile = pl.BlockSpec((block_q, width), lambda i, b: (i, 0))
    whole = pl.BlockSpec((length, width), lambda i, b: (0, 0))
    row = pl.BlockSpec((1, block_q), lambda i, b: (0, i))
    return pl.pallas_call(
        attend_kernel,
        name="attend",
        grid_spec=pltpu.PrefetchScalarGridSpec(
            num_scalar_prefetch=1,
            grid=(length // block_q,),
            in_specs=[
                tile,
                whole,
                whole,
                row,
                pl.BlockSpec((length, 1), lambda i, b: (0, 0)),
            ],
            out_specs=[tile, tile, pl.BlockSpec((heads, block_q), lambda i, b: (0, i))],
            scratch_shapes=[pltpu.VMEM((heads, length, HD), half)] * 2,
        ),
        out_shape=[
            jax.ShapeDtypeStruct((length, width), half),
            jax.ShapeDtypeStruct((length, width), single),
            jax.ShapeDtypeStruct((heads, length), single),
        ],
    )(bounds, query, key, value, seg_row, seg_col)


def attend_backward(query, key, value, grad, context, logsum, plan):
    bounds, seg_row, seg_col = plan
    length, width = query.shape
    heads = width // HD
    tile = pl.BlockSpec((block_q, width), lambda i, b: (i, 0))
    whole = pl.BlockSpec((length, width), lambda i, b: (0, 0))
    row = pl.BlockSpec((1, block_q), lambda i, b: (0, i))
    return pl.pallas_call(
        attend_back_kernel,
        name="attend_back",
        grid_spec=pltpu.PrefetchScalarGridSpec(
            num_scalar_prefetch=1,
            grid=(length // block_q,),
            in_specs=[
                tile,
                whole,
                whole,
                tile,
                tile,
                pl.BlockSpec((heads, block_q), lambda i, b: (0, i)),
                row,
                pl.BlockSpec((length, 1), lambda i, b: (0, 0)),
            ],
            out_specs=[tile, whole, whole, pl.BlockSpec((2, width), lambda i, b: (0, 0))],
            scratch_shapes=[
                pltpu.VMEM((heads, length, HD), half),
                pltpu.VMEM((heads, length, HD), half),
                pltpu.VMEM((heads, length, HD), single),
                pltpu.VMEM((heads, length, HD), single),
                pltpu.VMEM((1, width), single),
            ],
        ),
        out_shape=[
            jax.ShapeDtypeStruct((length, width), half),
            jax.ShapeDtypeStruct((length, width), half),
            jax.ShapeDtypeStruct((length, width), half),
            jax.ShapeDtypeStruct((2, width), single),
        ],
    )(bounds, query, key, value, grad, context, logsum, seg_row, seg_col)


def adamw_kernel(grad, param, moments, grad_out, param_out, moments_out):
    value = grad[...].astype(single)
    grad_out[...] = value
    first = beta_one * moments[0] + (1.0 - beta_one) * value
    second = beta_two * moments[1] + (1.0 - beta_two) * value * value
    update = (
        first
        / (1.0 - beta_one**adam_step)
        / (jnp.sqrt(second / (1.0 - beta_two**adam_step)) + adam_eps)
    )
    param_out[...] = param[...] - learning_rate * (update + weight_decay * param[...])
    moments_out[0] = first
    moments_out[1] = second


def adamw_matrix(grad, param, moments):
    shape = param.shape
    columns = shape[-1]
    rows = param.size // columns
    tile_rows = rows
    while tile_rows * columns > 131072 and tile_rows % 2 == 0:
        tile_rows //= 2
    tile = pl.BlockSpec((tile_rows, columns), lambda i: (i, 0))
    pair = pl.BlockSpec((2, tile_rows, columns), lambda i: (0, i, 0))
    grad_new, param_new, moments_new = pl.pallas_call(
        adamw_kernel,
        name="adamw",
        grid=(rows // tile_rows,),
        in_specs=[tile, tile, pair],
        out_specs=[tile, tile, pair],
        out_shape=[
            jax.ShapeDtypeStruct((rows, columns), single),
            jax.ShapeDtypeStruct((rows, columns), single),
            jax.ShapeDtypeStruct((2, rows, columns), single),
        ],
    )(
        grad.reshape(rows, columns),
        param.reshape(rows, columns),
        moments.reshape(2, rows, columns),
    )
    return (
        grad_new.reshape(shape),
        param_new.reshape(shape),
        moments_new.reshape((2,) + shape),
    )


def gather_shard(block, axis):
    rank = lax.axis_index("shard")
    count = block.shape[axis]
    across = lax.ppermute(block, "shard", chip_swap)
    beside = lax.ppermute(block, "shard", core_swap)
    corner = lax.ppermute(across, "shard", core_swap)
    shape = list(block.shape)
    shape[axis] = 4 * count
    full = jnp.zeros(shape, block.dtype)
    for offset, part in enumerate((block, beside, across, corner)):
        full = lax.dynamic_update_slice_in_dim(full, part, (rank ^ offset) * count, axis)
    return full


def exchange_context(blocks, axis):
    rank = lax.axis_index("context")
    result = blocks
    for hop in (2, 1, 3):
        ring = [(i, (i + hop) % 4) for i in range(4)]
        part = lax.dynamic_slice_in_dim(blocks, (rank + hop) % 4, 1, axis)
        part = lax.ppermute(part, "context", ring)
        result = lax.dynamic_update_slice_in_dim(result, part, (rank - hop) % 4, axis)
    return result


def pair_sum(part):
    part = part.astype(half)
    other = lax.ppermute(part, "tensor", pair_swap)
    return part.astype(single) + other.astype(single)


def sum_context(part):
    rank = lax.axis_index("context")
    inner = (rank == 1) | (rank == 2)
    side = lax.ppermute(part, "context", line_in)
    joined = (part.astype(single) + side.astype(single)).astype(half)
    other = lax.ppermute(joined, "context", line_mid)
    total = (joined.astype(single) + other.astype(single)).astype(half)
    back = lax.ppermute(total, "context", line_out)
    return jnp.where(inner, total, back)


def column_sets(rows):
    rank = lax.axis_index("shard")
    core = rank % 2
    blocks = rows.reshape(rows.shape[0], 2, 2, rows.shape[1] // 4)
    keep = lax.dynamic_slice_in_dim(blocks, core, 1, 2)
    send = lax.dynamic_slice_in_dim(blocks, 1 - core, 1, 2)
    return (
        keep.reshape(rows.shape[0], -1),
        send.reshape(rows.shape[0], -1),
    )


def scatter_shard(keep, send, axis):
    chip = lax.axis_index("shard") // 2
    other = lax.ppermute(send, "shard", core_swap)
    joined = (keep.astype(single) + other.astype(single)).astype(half)
    count = joined.shape[axis] // 2
    away = lax.dynamic_slice_in_dim(joined, (1 - chip) * count, count, axis)
    mine = lax.dynamic_slice_in_dim(joined, chip * count, count, axis)
    other = lax.ppermute(away, "shard", chip_swap)
    return (mine.astype(single) + other.astype(single)).astype(half)


def fast_mesh(
    layer_input,
    segment_ids,
    out_grad,
    attn_in,
    attn_out,
    mlp_up,
    mlp_down,
    vectors,
    up_bias,
    attn_in_moments,
    attn_out_moments,
    mlp_up_moments,
    mlp_down_moments,
    vector_moments,
    up_bias_moments,
):
    tensor_rank = lax.axis_index("tensor")
    context_rank = lax.axis_index("context")
    contexts = lax.axis_size("context")
    tokens = layer_input[0]
    count_rows, model_width = tokens.shape
    share_rows = out_grad.shape[1]
    head_width = attn_in.shape[2]
    hidden_width = mlp_up.shape[1]
    length = segment_ids.shape[1]
    group = head_width // contexts
    plan = attention_plan(segment_ids[0])
    in_full = gather_shard(attn_in.astype(half), 1)
    out_full = gather_shard(attn_out.astype(half), 1)
    up_full = gather_shard(mlp_up.astype(half), 0)
    down_full = gather_shard(mlp_down.astype(half), 1)
    upstream_other = lax.ppermute(out_grad[0], "tensor", pair_swap)
    upstream_half = jnp.where(
        tensor_rank == 0,
        jnp.concatenate([out_grad[0], upstream_other], 0),
        jnp.concatenate([upstream_other, out_grad[0]], 0),
    )
    upstream = upstream_half.astype(single)
    tokens_all = lax.all_gather(tokens, "context", axis=0, tiled=True)
    head_start = tensor_rank * head_width
    unit_start = tensor_rank * hidden_width
    query_bias = lax.dynamic_slice_in_dim(vectors[0], head_start, head_width)
    value_bias = lax.dynamic_slice_in_dim(vectors[1], head_start, head_width)
    unit_bias = lax.dynamic_slice_in_dim(up_bias, unit_start, hidden_width)
    bias = jnp.stack([query_bias, jnp.zeros_like(query_bias), value_bias])
    project = jnp.einsum("td,kdh->kth", tokens, in_full, preferred_element_type=single)
    project = (project + bias[:, None]).astype(half)
    project = project.reshape(3, count_rows, contexts, group).transpose(2, 0, 1, 3)
    mine = exchange_context(project, 0)
    mine = mine.transpose(1, 0, 2, 3).reshape(3, length, group)
    query, key, value = mine[0], mine[1], mine[2]
    attended, context, logsum = attend_forward(query, key, value, plan)
    context_half = exchange_context(attended.reshape(contexts, count_rows, group), 0)
    context_half = context_half.transpose(1, 0, 2).reshape(count_rows, head_width)
    attn = pair_sum(jnp.dot(context_half, out_full, preferred_element_type=single))
    normed_one, scale_one = normalize(tokens.astype(single) + attn + vectors[2])
    first = normed_one * vectors[4] + vectors[5]
    first_half = first.astype(half)
    before = jnp.dot(first_half, up_full, preferred_element_type=single) + unit_bias
    hidden_half = gelu_value(before).astype(half)
    mlp = pair_sum(jnp.dot(hidden_half, down_full, preferred_element_type=single))
    normed_two, scale_two = normalize(first + mlp + vectors[3])
    own_rows = lax.dynamic_slice_in_dim(normed_two, tensor_rank * share_rows, share_rows)
    block_output = (own_rows * vectors[6] + vectors[7]).astype(half)
    grad_two = norm_back(upstream, normed_two, scale_two, vectors[6])
    grad_two_half = grad_two.astype(half)
    grad_before = against_rows(grad_two_half, down_full) * gelu_slope(before)
    grad_before_half = grad_before.astype(half)
    grad_first = grad_two + pair_sum(against_rows(grad_before_half, up_full))
    grad_one = norm_back(grad_first, normed_one, scale_one, vectors[4])
    grad_one_half = grad_one.astype(half)
    grad_context = jnp.einsum(
        "td,gcd->gtc",
        grad_one_half,
        out_full.reshape(contexts, group, model_width),
        preferred_element_type=single,
    ).astype(half)
    grad_mine = exchange_context(grad_context, 0).reshape(length, group)

    keep, send = column_sets(grad_two_half)
    down_own = scatter_shard(
        inner_rows(hidden_half, keep).astype(half), inner_rows(hidden_half, send).astype(half), 1
    )
    keep, send = column_sets(first_half)
    up_own = scatter_shard(
        inner_rows(keep, grad_before_half).astype(half),
        inner_rows(send, grad_before_half).astype(half),
        0,
    )
    keep, send = column_sets(grad_one_half)
    out_own = scatter_shard(
        inner_rows(context_half, keep).astype(half), inner_rows(context_half, send).astype(half), 1
    )
    down_sum, down_new, down_moments = adamw_matrix(
        sum_context(down_own), mlp_down, mlp_down_moments
    )
    up_sum, up_new, up_moments = adamw_matrix(sum_context(up_own), mlp_up, mlp_up_moments)
    out_sum, out_new, out_moments = adamw_matrix(sum_context(out_own), attn_out, attn_out_moments)

    query_grad, key_grad, value_grad, head_sums = attend_backward(
        query, key, value, grad_mine, context, logsum, plan
    )
    stacked = jnp.concatenate([query_grad, key_grad, value_grad], 1)
    keep, send = column_sets(tokens_all)
    in_own = scatter_shard(
        inner_rows(keep, stacked).astype(half), inner_rows(send, stacked).astype(half), 0
    )
    in_all = lax.all_gather(in_own, "context", axis=0, tiled=False)
    in_all = in_all.reshape(contexts, attn_in.shape[1], 3, group).transpose(2, 1, 0, 3)
    in_sum, in_new, in_moments = adamw_matrix(
        in_all.reshape(attn_in.shape), attn_in, attn_in_moments
    )
    blocks = jnp.stack([query_grad, key_grad, value_grad]).reshape(3, contexts, count_rows, group)
    blocks = exchange_context(blocks, 1)
    blocks = blocks.transpose(0, 2, 1, 3).reshape(3, count_rows, head_width)
    share = jnp.einsum("kth,kdh->td", blocks, in_full, preferred_element_type=single).astype(half)
    share_mine = lax.dynamic_slice_in_dim(share, tensor_rank * share_rows, share_rows)
    share_away = lax.dynamic_slice_in_dim(share, (1 - tensor_rank) * share_rows, share_rows)
    share_away = lax.ppermute(share_away, "tensor", pair_swap)
    grad_one_mine = lax.dynamic_slice_in_dim(grad_one, tensor_rank * share_rows, share_rows)
    input_grad = (
        grad_one_mine + share_mine.astype(single) + share_away.astype(single)
    ).astype(half)

    group_start = head_start + context_rank * group
    head_rows = lax.dynamic_update_slice(
        jnp.zeros((2, model_width), single), head_sums, (0, group_start)
    )
    shared_rows = 0.5 * jnp.stack(
        [
            jnp.sum(grad_one, 0),
            jnp.sum(grad_two, 0),
            jnp.sum(grad_first * normed_one, 0),
            jnp.sum(grad_first, 0),
            jnp.sum(upstream * normed_two, 0),
            jnp.sum(upstream, 0),
        ]
    )
    local_bias = lax.dynamic_update_slice(
        jnp.zeros((up_bias.shape[0],), single), jnp.sum(grad_before, 0), (unit_start,)
    )
    local = jnp.concatenate(
        [head_rows, shared_rows, local_bias.reshape(-1, model_width)], 0
    )
    everyone = lax.all_gather(local, ("shard", "context", "tensor"), axis=0, tiled=False)
    everyone = jnp.sum(everyone, 0)
    vector_grad = everyone[:8]
    bias_grad = everyone[8:].reshape(up_bias.shape)
    vec_new, vec_moments = adamw(vectors, vector_moments, vector_grad, 0.0)
    bias_new, bias_moments = adamw(up_bias, up_bias_moments, bias_grad, 0.0)
    return (
        block_output[None],
        input_grad[None],
        in_sum,
        out_sum,
        up_sum,
        down_sum,
        vector_grad,
        bias_grad,
        in_new,
        out_new,
        up_new,
        down_new,
        vec_new,
        bias_new,
        in_moments,
        out_moments,
        up_moments,
        down_moments,
        vec_moments,
        bias_moments,
    )


def solution(mesh):
    in_specs = (
        P("shard", "context", None),
        P("shard", None),
        P("shard", ("context", "tensor"), None),
        P(None, "shard", "tensor"),
        P("tensor", "shard"),
        P("shard", "tensor"),
        P("tensor", "shard"),
        P(),
        P(),
        P(None, None, "shard", "tensor"),
        P(None, "tensor", "shard"),
        P(None, "shard", "tensor"),
        P(None, "tensor", "shard"),
        P(),
        P(),
    )
    out_specs = (
        P("shard", ("context", "tensor"), None),
        P("shard", ("context", "tensor"), None),
        P(None, "shard", "tensor"),
        P("tensor", "shard"),
        P("shard", "tensor"),
        P("tensor", "shard"),
        P(),
        P(),
        P(None, "shard", "tensor"),
        P("tensor", "shard"),
        P("shard", "tensor"),
        P("tensor", "shard"),
        P(),
        P(),
        P(None, None, "shard", "tensor"),
        P(None, "tensor", "shard"),
        P(None, "shard", "tensor"),
        P(None, "tensor", "shard"),
        P(),
        P(),
    )
    on_device = fast_mesh if fits(mesh) else any_mesh
    return jax.shard_map(
        on_device, mesh=mesh, in_specs=in_specs, out_specs=out_specs, check_vma=False
    )
```
